32 devices in a mesh: grp: 4 (over y, x), fsdp: 8 (over z, core).
Axes of the slice: x: 2, y: 2, z: 4, core: 2. Of those that a mesh axis runs over, the one named last changes fastest.
Arguments:
- tokens: bfloat16 [8192, 8192], P(('grp', 'fsdp')), may hold values from -6 to 6
- cotangent: bfloat16 [8192, 16384], P(('grp', 'fsdp')), may hold values from -6 to 6
- adapter_a: float32 [16, 16, 8192], P(None, None, 'fsdp'), may hold values from -0.0625 to 0.0625
- adapter_b: float32 [16, 16, 16384], P(None, None, 'fsdp'), may hold values from -1.5 to 1.5
- block_map: int32 [64], replicated, may hold values from 0 to 15, as said below
- adapter_owner: int32 [16], replicated, may hold values from 0 to 3, as said below
Outputs:
- delta: bfloat16 [8192, 16384], P(('grp', 'fsdp'))
- grad_tokens: bfloat16 [8192, 8192], P(('grp', 'fsdp'))
- grad_down: float32 [32, 16, 8192], P('grp', None, 'fsdp')
- grad_up: float32 [32, 16, 16384], P('grp', None, 'fsdp')
The draws below stay inside these ranges and needn't reach their ends.
Inputs may be any that keep to these rules, and one draw needn't show every extreme that they name: `block_map`: the 16 blocks of each group (blocks g * 16 to (g + 1) * 16 - 1) name exactly 4 distinct adapters. `adapter_owner`: no group owns more than 8 adapters, and one group owns exactly 8.
All inputs are finite; a program needn't handle non-finite values.
Results may differ from the reference program's by a relative error of at most 0.0065.
Values may be sent and summed in bfloat16 or wider, within the bound.
A program may use at most 128 MiB of HBM per device.

```python
import jax
import jax.numpy as jnp
from jax import lax

D = 8192
HID = 16384
RANK = 16
BLOCK = 128
ADAPTERS = 16
USED = 4
OWN_MAX = 8
BLK_GRP = 16
BLOCKS = 64
TOKENS = 8192
N_GRP = 4


def draw_block_map(key, part):

    def one_group(group_id):
        group_key = jax.random.fold_in(key, group_id)
        subkeys = jax.random.split(group_key, 3)
        chosen = jax.random.permutation(subkeys[0], ADAPTERS)[:USED]
        assigned = jax.random.randint(subkeys[1], (BLK_GRP,), 0, USED)
        assigned = assigned.at[:USED].set(jnp.arange(USED))
        assigned = assigned[jax.random.permutation(subkeys[2], BLK_GRP)]
        return chosen[assigned].astype(jnp.int32)
    return jax.vmap(one_group)(jnp.arange(N_GRP)).reshape(BLOCKS).astype(jnp.int32)


def draw_adapter_owner(key, part):
    subkeys = jax.random.split(jax.random.fold_in(key, 7), 3)
    shuffled = jax.random.permutation(subkeys[0], ADAPTERS)
    heavy_group = jax.random.randint(subkeys[1], (), 0, N_GRP)
    others = jax.random.randint(subkeys[2], (ADAPTERS,), 0, N_GRP - 1)
    others = others + (others >= heavy_group).astype(jnp.int32)
    ranked = jnp.where(jnp.arange(ADAPTERS) < OWN_MAX, heavy_group, others).astype(jnp.int32)
    return jnp.zeros((ADAPTERS,), jnp.int32).at[shuffled].set(ranked)


def block_levels(key, shape, cuts, low, largest):
    def one(axis_at, blocks):
        heights = jax.random.uniform(jax.random.fold_in(jax.random.fold_in(key, 6), axis_at), (blocks,), jnp.float32, low / len(cuts), largest / len(cuts))
        return jnp.repeat(jnp.exp(heights), shape[axis_at] // blocks).reshape((-1,) + (1,) * (len(shape) - axis_at - 1))

    level = one(*cuts[0])
    for cut in cuts[1:]:
        level = level * one(*cut)
    return level


def gaussian(key, shape, scale, reach, cuts=(), held_as=jnp.bfloat16):
    level = block_levels(key, shape, cuts, -0.22, 0.18) if cuts else 1.0
    entries = jax.random.normal(key, shape, jnp.float32) * scale * level
    return jnp.minimum(jnp.maximum(entries, -reach), reach).astype(held_as)


def setup_inputs(seed: int = 0) -> dict:
    splits = jax.random.split(jax.random.key(seed), 7)
    return {
        "tokens": gaussian(splits[0], (TOKENS, D), 1.0, 6.0, ((0, 32),)),
        "cotangent": gaussian(splits[1], (TOKENS, HID), 1.0, 6.0, ((0, 32),)),
        "adapter_a": gaussian(splits[2], (ADAPTERS, RANK, D), D ** -0.5, 0.0625, ((2, 8),), jnp.float32),
        "adapter_b": gaussian(splits[3], (ADAPTERS, RANK, HID), RANK ** -0.5, 1.5, ((2, 8),), jnp.float32),
        "block_map": draw_block_map(jax.random.fold_in(splits[6], 71), 0),
        "adapter_owner": draw_adapter_owner(jax.random.fold_in(splits[6], 71), 0),
    }


def ordered_members(members, slot_count):
    total = members.shape[-1]
    position = (jnp.cumsum(members, axis=-1) - 1).astype(jnp.int32)
    slot_range = jnp.arange(slot_count, dtype=jnp.int32)
    matches = (members[..., None, :] == 1) & (position[..., None, :] == slot_range[:, None])
    catalog = jnp.arange(total, dtype=jnp.int32)
    found = jnp.sum(jnp.where(matches, catalog, 0), axis=-1).astype(jnp.int32)
    return jnp.where(jnp.any(matches, axis=-1), found, -1).astype(jnp.int32)


def reference(tokens, cotangent, adapter_a, adapter_b, block_map, adapter_owner):
    down_low = adapter_a.astype(jnp.bfloat16)
    up_low = adapter_b.astype(jnp.bfloat16)
    blocks = block_map.shape[0]
    tok_blocks = tokens.reshape(blocks, BLOCK, D)
    cot_blocks = cotangent.reshape(blocks, BLOCK, HID)

    def advance(totals, pieces):
        sum_a, sum_b = totals
        tok_piece, cot_piece, adapter_id = pieces
        down_one = down_low[adapter_id]
        up_one = up_low[adapter_id]
        low_rank = jnp.dot(tok_piece, down_one.T, preferred_element_type=jnp.float32).astype(jnp.bfloat16)
        delta_piece = jnp.dot(low_rank, up_one, preferred_element_type=jnp.float32).astype(jnp.bfloat16)
        back_rank = jnp.dot(cot_piece, up_one.T, preferred_element_type=jnp.float32).astype(jnp.bfloat16)
        grad_piece = jnp.dot(back_rank, down_one, preferred_element_type=jnp.float32).astype(jnp.bfloat16)
        down_part = jnp.dot(back_rank.T, tok_piece, preferred_element_type=jnp.float32)
        up_part = jnp.dot(low_rank.T, cot_piece, preferred_element_type=jnp.float32)
        sum_a = sum_a.at[adapter_id].add(down_part)
        sum_b = sum_b.at[adapter_id].add(up_part)
        return (sum_a, sum_b), (delta_piece, grad_piece)

    start_a = jnp.zeros((ADAPTERS, RANK, D), jnp.float32)
    start_b = jnp.zeros((ADAPTERS, RANK, HID), jnp.float32)
    (sum_a, sum_b), (delta_blocks, grad_blocks) = lax.scan(
        advance, (start_a, start_b), (tok_blocks, cot_blocks, block_map.astype(jnp.int32)))
    catalog = jnp.arange(ADAPTERS, dtype=jnp.int32)
    uses = jnp.sum((block_map[:, None] == catalog[None, :]).astype(jnp.int32), axis=0).astype(jnp.int32)
    divisor = (BLOCK * jnp.maximum(uses, 1)).astype(jnp.float32)
    sum_down = sum_a / divisor[:, None, None]
    sum_up = sum_b / divisor[:, None, None]
    owner_marks = (adapter_owner[None, :] == jnp.arange(N_GRP, dtype=jnp.int32)[:, None]).astype(jnp.int32)
    owned = ordered_members(owner_marks, OWN_MAX).reshape(N_GRP * OWN_MAX)
    filled = (owned >= 0).astype(jnp.float32)
    safe_ids = jnp.maximum(owned, 0).astype(jnp.int32)
    grad_down = sum_down[safe_ids] * filled[:, None, None]
    grad_up = sum_up[safe_ids] * filled[:, None, None]
    delta = delta_blocks.reshape(blocks * BLOCK, HID)
    grad_tokens = grad_blocks.reshape(blocks * BLOCK, D)
    return (delta, grad_tokens, grad_down, grad_up)
```

```python
import functools

import jax
import jax.numpy as jnp
from jax import lax
from jax.experimental import pallas as pl
from jax.experimental.pallas import tpu as pltpu
from jax.sharding import PartitionSpec as P

BLOCK = 128
USED = 4
OWN_MAX = 8
RANK = 16
ROWS = USED * RANK
MESH = pl.DeviceIdType.MESH
NT = (((1,), (1,)), ((), ()))
PIECES = 3
RIGHT, LEFT, PARTNER = 0, 1, 2


def used_adapters(bm, base, count, last_name):
    found = []
    for _ in range(USED):
        def smallest(i, best, last=found[-1] if found else -1):
            entry = bm[base + i]
            return jnp.where((entry > last) & (entry < best), entry, best)

        found.append(lax.fori_loop(0, count, smallest, jnp.int32(last_name), unroll=min(count, 16)))
    return found


def exchange(
    groups, shards,
    bm, owners, a_hbm, b_hbm,
    mask_out, pick_out, scale_out, wd_out, wu_out,
    a_f32, b_f32, wd, wu, load_sem, store_sem, ag_send, ag_recv,
):
    line = shards // 2
    g = lax.axis_index("grp")
    f = lax.axis_index("fsdp")
    z = f // 2
    c = f % 2
    mate = z * 2 + (1 - c)
    wp = a_hbm.shape[2]
    rows = mask_out.shape[0]
    blocks_dev = rows // BLOCK
    total_blocks = bm.shape[0]
    group_blocks = total_blocks // groups
    adapters = a_hbm.shape[0]

    barrier = pltpu.get_barrier_semaphore()
    pl.semaphore_signal(barrier, inc=1, device_id=(g, mate), device_id_type=MESH)
    for step in range(1, line):
        pl.semaphore_signal(
            barrier, inc=1, device_id=(g, ((z + step) % line) * 2 + c), device_id_type=MESH
        )
    for step in range(1, groups):
        pl.semaphore_signal(
            barrier, inc=1, device_id=((g + step) % groups, f), device_id_type=MESH
        )
    load_a = pltpu.make_async_copy(a_hbm, a_f32, load_sem.at[0])
    load_b = pltpu.make_async_copy(b_hbm, b_f32, load_sem.at[1])
    load_a.start()
    load_b.start()

    used = used_adapters(bm, g * group_blocks, group_blocks, adapters - 1)

    def weights(piece, shard):
        return wd.at[shard] if piece == 0 else wu.at[piece - 1, shard]

    endings = []

    def send(cond, build):
        if cond is None:
            build().start()
            endings.append(lambda: build().wait_send())
            return

        @pl.when(cond)
        def _():
            build().start()

        def finish():
            @pl.when(cond)
            def _():
                build().wait_send()

        endings.append(finish)

    def gather_copy(piece, origin, way):
        ref = weights(piece, origin)
        target = {RIGHT: f + 2, LEFT: f - 2, PARTNER: mate}[way]
        return pltpu.make_async_remote_copy(
            src_ref=ref, dst_ref=ref,
            send_sem=ag_send.at[way, piece, origin // 2],
            recv_sem=ag_recv.at[piece, origin],
            device_id=(g, target), device_id_type=MESH,
        )

    def gather_send(piece, origin, way, cond):
        send(cond, lambda: gather_copy(piece, origin, way))

    def gather_own(piece):
        gather_send(piece, f, RIGHT, z < line - 1)
        gather_send(piece, f, LEFT, z > 0)
        gather_send(piece, f, PARTNER, None)

    def gather_step(piece, dist):
        for sign in (-1, 1):
            here = (z - dist >= 0) if sign < 0 else (z + dist < line)
            origin = (z + sign * dist) * 2 + c
            onward = (z < line - 1) if sign < 0 else (z > 0)

            @pl.when(here)
            def _():
                gather_copy(piece, origin, PARTNER).wait_recv()

            gather_send(piece, origin, RIGHT if sign < 0 else LEFT, here & onward)
            gather_send(piece, origin, PARTNER, here)
    def gather_mates(piece, dists):
        for dist in dists:
            for sign in (-1, 1) if dist else (1,):
                here = (z - dist >= 0) if sign < 0 else (z + dist < line)
                origin = (z + sign * dist) * 2 + (1 - c)

                @pl.when(here)
                def _():
                    gather_copy(piece, origin, PARTNER).wait_recv()

    def masked(acc):
        row = lax.broadcasted_iota(jnp.int32, (rows, ROWS), 0) // BLOCK
        slot = lax.broadcasted_iota(jnp.int32, (rows, ROWS), 1) // RANK
        wanted = jnp.zeros((rows, ROWS), jnp.int32)
        for b in range(blocks_dev):
            entry = bm[(g * shards + f) * blocks_dev + b]
            place = jnp.int32(0)
            for s in range(1, USED):
                place = jnp.where(entry == used[s], s, place)
            wanted = jnp.where(row == b, place, wanted)
        return jnp.where(slot == wanted, acc, 0.0)

    load_a.wait()
    wd[f] = jnp.concatenate([a_f32[u].astype(jnp.bfloat16) for u in used], axis=0)
    pl.semaphore_wait(barrier, line + groups - 1)
    gather_own(0)
    load_b.wait()
    for half in range(2):
        wu[half, f] = jnp.concatenate(
            [b_f32[u, :, half * wp:(half + 1) * wp].astype(jnp.bfloat16) for u in used], axis=0
        )
    for dist in range(1, line):
        gather_step(0, dist)
        if dist == 1:
            gather_own(1)
    for dist in range(1, line):
        gather_step(1, dist)
        if dist == 1:
            gather_own(2)
    for dist in range(1, line):
        gather_step(2, dist)
    for piece in range(PIECES):
        gather_mates(piece, range(line))
    mask_out[...] = masked(jnp.ones((rows, ROWS), jnp.float32))
    store_d = pltpu.make_async_copy(wd, wd_out, store_sem.at[0])
    store_u = pltpu.make_async_copy(wu, wu_out, store_sem.at[1])
    store_d.start()
    store_u.start()

    names = [
        used_adapters(bm, other * group_blocks, group_blocks, adapters - 1)
        for other in range(groups)
    ]
    owned = [jnp.int32(-1)] * OWN_MAX
    position = jnp.int32(0)
    for a in range(adapters):
        mine = owners[a] == g
        for k in range(OWN_MAX):
            owned[k] = jnp.where(mine & (position == k), a, owned[k])
        position = position + jnp.where(mine, 1, 0)

    def count(i, totals):
        entry = bm[i]
        return tuple(n + jnp.where(entry == o, 1, 0) for n, o in zip(totals, owned))

    totals = lax.fori_loop(0, total_blocks, count, (jnp.int32(0),) * OWN_MAX, unroll=8)
    shape = (OWN_MAX * RANK, groups * ROWS)
    row = lax.broadcasted_iota(jnp.int32, shape, 0)
    col = lax.broadcasted_iota(jnp.int32, shape, 1)
    row_name = jnp.full(shape, -1, jnp.int32)
    col_name = jnp.full(shape, -2, jnp.int32)
    for k in range(OWN_MAX):
        row_name = jnp.where(row // RANK == k, owned[k], row_name)
    for q in range(groups * USED):
        col_name = jnp.where(col // RANK == q, names[q // USED][q % USED], col_name)
    hit = (row % RANK == col % RANK) & (row_name == col_name)
    pick_out[...] = jnp.where(hit, 1.0, 0.0).astype(jnp.bfloat16)
    wide = lax.broadcasted_iota(jnp.int32, scale_out.shape, 0) // RANK
    uses = jnp.zeros(scale_out.shape, jnp.int32)
    for k in range(OWN_MAX):
        uses = jnp.where(wide == k, totals[k], uses)
    scale_out[...] = 1.0 / (BLOCK * jnp.maximum(uses, 1)).astype(jnp.float32)
    store_d.wait()
    store_u.wait()
    for finish in endings:
        finish()


def outputs(low, back, pick, scale, wd, wu, gd, gu, delta, grad_tokens, grad_down, grad_up):
    wp = wd.shape[2]
    for half in range(2):
        delta[:, half * wp:(half + 1) * wp] = jnp.dot(
            low[...], wu[half, 0], preferred_element_type=jnp.float32
        ).astype(delta.dtype)
    grad_tokens[...] = jnp.dot(back[...], wd[0], preferred_element_type=jnp.float32).astype(
        grad_tokens.dtype
    )

    @pl.when(pl.program_id(0) == 0)
    def _():
        for k in range(OWN_MAX):
            span = pl.ds(k * RANK, RANK)
            chosen, factor = pick[span, :], scale[span, 0:1]
            total = jnp.dot(chosen, gd[...], preferred_element_type=jnp.float32)
            grad_down[k] = total * factor
            for half in range(2):
                total = jnp.dot(chosen, gu[half], preferred_element_type=jnp.float32)
                grad_up[k, :, half * wp:(half + 1) * wp] = total * factor


def on_device(groups, shards, tokens, cotangent, adapter_a, adapter_b, block_map, adapter_owner):
    rows, width = tokens.shape
    hidden = cotangent.shape[1]
    wp = adapter_a.shape[2]
    assert adapter_b.shape[2] == 2 * wp
    line = shards // 2
    bf16, f32 = jnp.bfloat16, jnp.float32
    dma = pltpu.SemaphoreType.DMA
    vmem = pl.BlockSpec(memory_space=pltpu.VMEM)
    smem = pl.BlockSpec(memory_space=pltpu.SMEM)
    anywhere = pl.BlockSpec(memory_space=pl.ANY)
    mask, pick, scale, wd, wu = pl.pallas_call(
        functools.partial(exchange, groups, shards),
        name="exchange",
        out_shape=(
            jax.ShapeDtypeStruct((rows, ROWS), f32),
            jax.ShapeDtypeStruct((OWN_MAX * RANK, groups * ROWS), bf16),
            jax.ShapeDtypeStruct((OWN_MAX * RANK, 128), f32),
            jax.ShapeDtypeStruct((shards, ROWS, wp), bf16),
            jax.ShapeDtypeStruct((2, shards, ROWS, wp), bf16),
        ),
        in_specs=[smem, smem] + [anywhere] * 2,
        out_specs=(vmem, vmem, vmem, anywhere, anywhere),
        scratch_shapes=[
            pltpu.VMEM(adapter_a.shape, f32),
            pltpu.VMEM(adapter_b.shape, f32),
            pltpu.VMEM((shards, ROWS, wp), bf16),
            pltpu.VMEM((2, shards, ROWS, wp), bf16),
            dma((2,)),
            dma((2,)),
            dma((3, PIECES, line)),
            dma((PIECES, shards)),
        ],
        compiler_params=pltpu.CompilerParams(
            collective_id=0, has_side_effects=True, vmem_limit_bytes=58 * 1024 * 1024
        ),
    )(block_map, adapter_owner, adapter_a, adapter_b)
    down = wd.transpose(1, 0, 2).reshape(ROWS, width)
    up = wu.transpose(2, 1, 0, 3).reshape(ROWS, hidden)
    on = mask > 0.5

    def ranks(values, maps):
        total = lax.dot_general(values, maps, NT, preferred_element_type=f32)
        return jnp.where(on, total, 0.0).astype(bf16)

    def summed(left, values, size):
        part = lax.dot_general(
            left, values, (((0,), (0,)), ((), ())), preferred_element_type=f32
        ).astype(bf16)
        part = part.reshape(ROWS, shards, size).transpose(1, 0, 2)
        share = lax.psum_scatter(part, "fsdp", scatter_dimension=0, tiled=True)
        return lax.all_gather(share[0], "grp", axis=0)

    low = ranks(tokens, down)
    back = ranks(cotangent, up)
    gd = summed(back, tokens, wp)
    gu = summed(low, cotangent, 2 * wp).reshape(groups, ROWS, 2, wp).transpose(2, 0, 1, 3)
    gd = gd.reshape(groups * ROWS, wp)
    gu = gu.reshape(2, groups * ROWS, wp)
    whole = lambda shape: pl.BlockSpec(shape, lambda i: (0,) * len(shape))
    delta, grad_tokens, grad_down, grad_up = pl.pallas_call(
        outputs,
        name="outputs",
        grid=(shards,),
        out_shape=(
            jax.ShapeDtypeStruct((rows, hidden), bf16),
            jax.ShapeDtypeStruct((rows, width), bf16),
            jax.ShapeDtypeStruct((OWN_MAX, RANK, wp), f32),
            jax.ShapeDtypeStruct((OWN_MAX, RANK, 2 * wp), f32),
        ),
        in_specs=[
            whole(low.shape), whole(back.shape), whole(pick.shape), whole(scale.shape),
            pl.BlockSpec((1, ROWS, wp), lambda i: (i, 0, 0)),
            pl.BlockSpec((2, 1, ROWS, wp), lambda i: (0, i, 0, 0)),
            whole(gd.shape), whole(gu.shape),
        ],
        out_specs=(
            pl.BlockSpec((rows, 2 * wp), lambda i: (0, i)),
            pl.BlockSpec((rows, wp), lambda i: (0, i)),
            whole((OWN_MAX, RANK, wp)), whole((OWN_MAX, RANK, 2 * wp)),
        ),
    )(low, back, pick, scale, wd, wu, gd, gu)
    return delta, grad_tokens, grad_down, grad_up


def solution(mesh):
    placed = (
        P(("grp", "fsdp"), None),
        P(("grp", "fsdp"), None),
        P(None, None, "fsdp"),
        P(None, None, "fsdp"),
        P(),
        P(),
    )
    return jax.shard_map(
        functools.partial(on_device, mesh.shape["grp"], mesh.shape["fsdp"]),
        mesh=mesh,
        in_specs=placed,
        out_specs=(
            P(("grp", "fsdp"), None),
            P(("grp", "fsdp"), None),
            P("grp", None, "fsdp"),
            P("grp", None, "fsdp"),
        ),
        check_vma=False,
    )
```
